32 devices in a mesh: helper: 16 (over z, x, core), tensor: 2 (over y).
Axes of the slice: x: 2, y: 2, z: 4, core: 2. Of those that a mesh axis runs over, the one named last changes fastest.
Arguments:
- recorded_input_rows: bfloat16 [16384, 2048], P('helper'), may hold values from -8 to 8
- out_cotangent: bfloat16 [16384, 2048], P('helper'), may hold values from -0.875 to 0.875
- fresh_rows: bfloat16 [4096, 2048], P('helper'), may hold values from -6 to 6
- seq_counts: int32 [16], replicated, may hold values from 1 to 4, 24 in all
- decay_logs: float32 [16, 256], P('tensor'), may hold values from -3 to 0
- norm_gain: float32 [2048], P('tensor'), may hold values from 0.25 to 1.75
- qkv_weight: float32 [2048, 3, 2048], P('helper', None, 'tensor'), may hold values from -0.125 to 0.125
- emitted_projection_matrix: float32 [2048, 2048], P('helper', 'tensor'), may hold values from -0.125 to 0.125
- qkv_first: float32 [2048, 3, 2048], P('helper', None, 'tensor'), may hold values from -6 to 6
- qkv_second: float32 [2048, 3, 2048], P('helper', None, 'tensor'), may hold values from 1 to 100
- out_first: float32 [2048, 2048], P('helper', 'tensor'), may hold values from -6 to 6
- out_second: float32 [2048, 2048], P('helper', 'tensor'), may hold values from 1 to 100
Outputs:
- fresh_out: bfloat16 [4096, 2048], P('helper')
- qkv_moment: float32 [2048, 3, 2048], P('helper', None, 'tensor')
- out_moment: float32 [2048, 2048], P('helper', 'tensor')
The draws below stay inside these ranges and needn't reach their ends.
Inputs may be any that keep to these rules, and one draw needn't show every extreme that they name: Helper h's live sequences are its first seq_counts[h] slots; the counts sum to three halves of the number of helpers, and the largest equals 4.
All inputs are finite; a program needn't handle non-finite values.
Results may differ from the reference program's by a relative error of at most 0.0095.
The reference program's roundings to bfloat16 on the way count: a program that leaves them out, or rounds other values in their place, can miss the bound.
Values may be sent and summed in bfloat16 or wider, within the bound.
A program may use at most 128 MiB of HBM per device.

```python
import math
import jax
import jax.numpy as jnp
import numpy as np
from jax import lax

HEADS = 16
D = 2048
SEQ_LEN = 256
SEQ_CAP = 4
N_HELPER = 16


def draw_decay_logs(key, part):
    key_rate = jax.random.fold_in(key, 11)
    key_place = jax.random.fold_in(key, 12)
    key_loss = jax.random.fold_in(key, 13)
    low_log = jnp.log(0.1 / SEQ_LEN)
    high_log = jnp.log(1.0 / 30.0)
    channel_fading_multiplier = jnp.exp(jax.random.uniform(key_rate, (HEADS, 1), jnp.float32, low_log, high_log))
    bucket_addresses = jax.random.randint(key_place, (HEADS, 3), 0, SEQ_LEN)
    objective_readings = jax.random.uniform(key_loss, (HEADS, 3), jnp.float32, 0.2, 0.5)
    element_indices = jnp.arange(SEQ_LEN)
    run_extent_list = jnp.sum(jnp.where(element_indices[None, None, :] == bucket_addresses[:, :, None], jnp.log(1.0 - objective_readings)[:, :, None], 0.0), axis=1)
    return (run_extent_list - channel_fading_multiplier).astype(jnp.float32)


def with_spikes(drawn, rng, source, target, parts, factor):
    owner, partner = [(jnp.arange(drawn.shape[position]) // (drawn.shape[position] // parts)).reshape([-1 if axis == position else 1 for axis in range(drawn.ndim)]) for position in (source, target)]
    chosen = jax.random.permutation(rng, parts)[partner]
    strong = (owner == chosen) | (owner == (partner + parts // 2) % parts)
    return jnp.where(strong, factor * drawn, drawn)


def shard_levels(stream_key, shape, cuts, smallest, high):
    gain = 1.0
    for dim, blocks in cuts:
        steps = jax.random.uniform(jax.random.fold_in(jax.random.fold_in(stream_key, 6), dim), (blocks,), jnp.float32, smallest / len(cuts), high / len(cuts))
        gain = gain * jnp.repeat(jnp.exp(steps), shape[dim] // blocks).reshape((-1,) + (1,) * (len(shape) - 1 - dim))
    return gain


def profile(count, total, bound, lean):
    loads = [(1 << 20) // math.isqrt(rank ** lean) + 1 for rank in range(2, count + 1)]
    rest, given = total - bound - (count - 1), [1] * (count - 1)
    while rest > 0:
        movable = [i for i in range(count - 1) if given[i] < bound]
        pool, left = sum([loads[i] for i in movable]), rest
        for i in movable:
            extra = min(bound - given[i], max(1, left * loads[i] // pool), rest)
            given[i] = given[i] + extra
            rest = rest - extra
    return np.array([bound] + given)


def uneven_parts(rng, count, total, limit, skew):
    if count == 2:
        one = jax.random.randint(rng, (), max(1, total - limit), min(limit, total - 1) + 1)
        return jnp.stack([one, total - one])
    sizes = jnp.asarray(profile(count, total, limit, skew), jnp.int32)
    twos = (count - 1) // 2
    donor, receiver = sizes[1:1 + 2 * twos:2], sizes[2:2 + 2 * twos:2]
    margin = jnp.minimum(donor - 1, limit - receiver)
    moved = jax.random.randint(jax.random.fold_in(rng, 1), (twos,), 0, 1 << 20) % (margin + 1)
    sizes = sizes.at[1:1 + 2 * twos:2].set(donor - moved).at[2:2 + 2 * twos:2].set(receiver + moved)
    return sizes[jax.random.permutation(jax.random.fold_in(rng, 2), count)]


def scatter_about(stream_key, extent, deviation, bound, cuts=(), kind=jnp.bfloat16):
    result = deviation * jax.random.normal(stream_key, extent, jnp.float32)
    if cuts:
        result = result * shard_levels(stream_key, extent, cuts, -0.22, 0.18)
    return jnp.clip(result, -bound, bound).astype(kind)


def heavy_noise(stream_key, shape, deviation, reach, shards, heavy, held_as=jnp.bfloat16):
    values = deviation * jax.random.normal(stream_key, shape, jnp.float32)
    if shards:
        values = values * shard_levels(stream_key, shape, shards, -0.22, 0.18)
    return jnp.clip(with_spikes(values, jax.random.fold_in(stream_key, 3), *heavy), -reach, reach).astype(held_as)


def setup_inputs(seed: int = 0) -> dict:
    key_list = jax.random.split(jax.random.key(seed), 13)
    recorded_input_rows = heavy_noise(key_list[0], (N_HELPER * SEQ_CAP * SEQ_LEN, D), 1.0, 8.0, ((0, 16),), (0, 1, 16, 2.0))
    out_cotangent = heavy_noise(key_list[1], (N_HELPER * SEQ_CAP * SEQ_LEN, D), 0.1, 0.875, ((0, 16),), (0, 1, 16, 2.0))
    fresh_rows = scatter_about(key_list[2], (N_HELPER * SEQ_LEN, D), 1.0, 6.0, ((0, 16),))
    seq_counts = uneven_parts(key_list[3], N_HELPER, 3 * N_HELPER // 2, SEQ_CAP, 2).astype(jnp.int32)
    decay_logs = draw_decay_logs(jax.random.fold_in(key_list[12], 71), 0)
    norm_gain = jnp.clip(1.0 + 0.15 * jax.random.normal(key_list[5], (D,), jnp.float32), 0.25, 1.75)
    qkv_weight = scatter_about(key_list[6], (D, 3, D), D ** -0.5, 0.125, ((0, 16), (2, 2)), jnp.float32)
    emitted_projection_matrix = scatter_about(key_list[7], (D, D), D ** -0.5, 0.125, ((0, 16), (1, 2)), jnp.float32)
    qkv_first = scatter_about(key_list[8], (D, 3, D), 1.0, 6.0, ((0, 16), (2, 2)), jnp.float32)
    qkv_second = jnp.clip(jnp.exp(math.log(100.0) - 4.6051702 * jax.random.uniform(key_list[9], (D, 3, D), jnp.float32) ** shard_levels(key_list[9], (D, 3, D), ((0, 16), (2, 2)), -0.2, 0.2)), 1.0, 100.0)
    out_first = scatter_about(key_list[10], (D, D), 1.0, 6.0, ((0, 16), (1, 2)), jnp.float32)
    out_second = jnp.clip(jnp.exp(math.log(100.0) - 4.6051702 * jax.random.uniform(key_list[11], (D, D), jnp.float32) ** shard_levels(key_list[11], (D, D), ((0, 16), (1, 2)), -0.2, 0.2)), 1.0, 100.0)
    return dict(recorded_input_rows=recorded_input_rows, out_cotangent=out_cotangent, fresh_rows=fresh_rows, seq_counts=seq_counts, decay_logs=decay_logs, norm_gain=norm_gain, qkv_weight=qkv_weight, emitted_projection_matrix=emitted_projection_matrix, qkv_first=qkv_first, qkv_second=qkv_second, out_first=out_first, out_second=out_second)


NORM_FLOOR = 1.0
BETA_ONE = 0.9
BETA_TWO = 0.95
ADAM_EPS = 1e-08
LEARN_RATE = 0.005
WEIGHT_DECAY = 0.1
BIAS_ONE = 0.9999734386011124
BIAS_TWO = 0.994079470779666

def product_of(form, left, right):
    return jnp.einsum(form, left.astype(jnp.float32), right.astype(jnp.float32))

def decay_table(decay_logs):
    running = jnp.cumsum(decay_logs.astype(jnp.float32), axis=1)
    length = decay_logs.shape[1]
    later = (jnp.arange(length)[:, None] >= jnp.arange(length)[None, :])[None]
    spread_factor = running[:, :, None] - running[:, None, :]
    return jnp.where(later, jnp.exp(jnp.where(later, spread_factor, 0.0)), 0.0)

def attend(projected, decay_mask, norm_gain):
    head_count = decay_mask.shape[0]
    split_shape = (projected.shape[0], projected.shape[1], head_count, projected.shape[3] // head_count)
    raw_query = projected[:, :, 0].reshape(split_shape)
    raw_key = projected[:, :, 1].reshape(split_shape)
    queries = (raw_query * jax.nn.sigmoid(raw_query)).astype(jnp.bfloat16)
    key_rows = (raw_key * jax.nn.sigmoid(raw_key)).astype(jnp.bfloat16)
    values = projected[:, :, 2].reshape(split_shape).astype(jnp.bfloat16)
    scores = product_of('sthd,suhd->shtu', queries, key_rows)
    weights = (scores * decay_mask[None]).astype(jnp.bfloat16)
    mixed = product_of('shtu,suhd->sthd', weights, values)
    mean_square = lax.optimization_barrier(jnp.mean(mixed * mixed, axis=-1, keepdims=True))
    active = jnp.where(mean_square > NORM_FLOOR, 1.0, 0.0)
    inverse = lax.rsqrt(jnp.maximum(mean_square, NORM_FLOOR))
    gain_heads = norm_gain.reshape(head_count, -1)
    attended = (mixed * inverse * gain_heads).astype(jnp.bfloat16)
    return (attended, (raw_query, raw_key, queries, key_rows, values, weights, mixed, inverse, active))

def attend_back(grad_attended, stashed, decay_mask, norm_gain):
    raw_query, raw_key, queries, key_rows, values, weights, mixed, inverse, active = stashed
    gain_heads = norm_gain.reshape(decay_mask.shape[0], -1)
    scaled = grad_attended * gain_heads
    grad_mixed = inverse * scaled - active * mixed * (inverse * inverse * inverse) * lax.optimization_barrier(jnp.mean(scaled * mixed, axis=-1, keepdims=True))
    grad_mixed = grad_mixed.astype(jnp.bfloat16)
    grad_weights = product_of('sthd,suhd->shtu', grad_mixed, values)
    grad_values = product_of('shtu,sthd->suhd', weights, grad_mixed)
    grad_scores = (grad_weights * decay_mask[None]).astype(jnp.bfloat16)
    grad_query = product_of('shtu,suhd->sthd', grad_scores, key_rows)
    grad_key = product_of('shtu,sthd->suhd', grad_scores, queries)
    sigma_query = jax.nn.sigmoid(raw_query)
    sigma_key = jax.nn.sigmoid(raw_key)
    grad_query = grad_query * sigma_query * (1.0 + raw_query * (1.0 - sigma_query))
    grad_key = grad_key * sigma_key * (1.0 + raw_key * (1.0 - sigma_key))
    return jnp.stack([grad_query, grad_key, grad_values], axis=2)

def adam_step(weight, first_moment, second_moment, gradient):
    first_new = BETA_ONE * first_moment + (1.0 - BETA_ONE) * gradient
    second_new = BETA_TWO * second_moment + (1.0 - BETA_TWO) * gradient * gradient
    update = first_new / BIAS_ONE / (jnp.sqrt(second_new / BIAS_TWO) + ADAM_EPS)
    weight_new = weight - LEARN_RATE * (update + WEIGHT_DECAY * weight)
    return (weight_new.astype(jnp.bfloat16), first_new)

def reference(recorded_input_rows, out_cotangent, fresh_rows, seq_counts, decay_logs, norm_gain, qkv_weight, emitted_projection_matrix, qkv_first, qkv_second, out_first, out_second):
    decay_mask = decay_table(decay_logs)
    model_width = qkv_weight.shape[0]
    head_count = decay_logs.shape[0]
    slot_total = recorded_input_rows.shape[0] // SEQ_LEN
    old_qkv = qkv_weight.astype(jnp.bfloat16).reshape(model_width, 3 * model_width)
    old_out = emitted_projection_matrix.astype(jnp.bfloat16)
    slot_index = (jnp.arange(slot_total) % SEQ_CAP).astype(jnp.int32)
    slot_limit = jnp.repeat(seq_counts.astype(jnp.int32), SEQ_CAP)
    slot_live = (slot_index < slot_limit).astype(jnp.float32)
    logged_seqs = recorded_input_rows.reshape(slot_total, SEQ_LEN, model_width)
    cot_seqs = out_cotangent.reshape(slot_total, SEQ_LEN, model_width)

    def replay_one(totals, inputs):
        seq_rows, seq_cot, live_flag = inputs

        def live_branch(partial_sums):
            projected = jnp.dot(seq_rows, old_qkv, preferred_element_type=jnp.float32).reshape(1, SEQ_LEN, 3, model_width)
            attended, stashed = attend(projected, decay_mask, norm_gain)
            grad_attended = jnp.dot(seq_cot, old_out, preferred_element_type=jnp.float32).reshape(1, SEQ_LEN, head_count, -1)
            grad_projected = attend_back(grad_attended, stashed, decay_mask, norm_gain)
            grad_projected = grad_projected.reshape(SEQ_LEN, 3 * model_width).astype(jnp.bfloat16)
            qkv_sum = partial_sums[0] + jnp.dot(seq_rows.T, grad_projected, preferred_element_type=jnp.float32)
            out_sum = partial_sums[1] + jnp.dot(seq_cot.T, attended.reshape(SEQ_LEN, model_width), preferred_element_type=jnp.float32)
            return (qkv_sum, out_sum)

        def inactive_branch(partial_sums):
            return partial_sums
        return (lax.cond(live_flag > 0.5, live_branch, inactive_branch, totals), None)
    start_sums = (jnp.zeros((model_width, 3 * model_width), jnp.float32), jnp.zeros((model_width, model_width), jnp.float32))
    prefix_accumulated = lax.scan(replay_one, start_sums, (logged_seqs, cot_seqs, slot_live))
    qkv_grad, out_grad = prefix_accumulated[0]
    new_qkv, qkv_moment = adam_step(qkv_weight, qkv_first, qkv_second, qkv_grad.reshape(model_width, 3, model_width))
    new_out, out_moment = adam_step(emitted_projection_matrix, out_first, out_second, out_grad)
    fresh_qkv = new_qkv.reshape(model_width, 3 * model_width)

    def recomputed_single(seq_rows):
        projected = jnp.dot(seq_rows, fresh_qkv, preferred_element_type=jnp.float32).reshape(1, SEQ_LEN, 3, model_width)
        attended = attend(projected, decay_mask, norm_gain)[0].reshape(SEQ_LEN, model_width)
        summed = seq_rows.astype(jnp.float32) + jnp.dot(attended, new_out.T, preferred_element_type=jnp.float32)
        return summed.astype(jnp.bfloat16)
    fresh_out = lax.map(recomputed_single, fresh_rows.reshape(-1, SEQ_LEN, model_width)).reshape(-1, model_width)
    return (fresh_out, qkv_moment, out_moment)
```

```python
import jax
import jax.numpy as jnp
from jax import lax
from jax.experimental import pallas as pl
from jax.experimental.pallas import tpu as pltpu
from jax.sharding import PartitionSpec as P


SEQ_LEN = 256


NORM_FLOOR = 1.0
BETA_ONE = 0.9
BETA_TWO = 0.95
ADAM_EPS = 1e-08
LEARN_RATE = 0.005
WEIGHT_DECAY = 0.1
BIAS_ONE = 0.9999734386011124
BIAS_TWO = 0.994079470779666


def product_of(form, left, right):
    return jnp.einsum(form, left, right, preferred_element_type=jnp.float32)


def decay_table(decay_logs):
    running = jnp.cumsum(decay_logs, axis=1)
    length = decay_logs.shape[1]
    later = (jnp.arange(length)[:, None] >= jnp.arange(length)[None, :])[None]
    spread_factor = running[:, :, None] - running[:, None, :]
    return jnp.where(later, jnp.exp(jnp.where(later, spread_factor, 0.0)), 0.0)


def attend(raw_query, raw_key, raw_value, decay_mask, norm_gain):
    head_count = decay_mask.shape[0]
    queries = (raw_query * jax.nn.sigmoid(raw_query)).astype(jnp.bfloat16)
    key_rows = (raw_key * jax.nn.sigmoid(raw_key)).astype(jnp.bfloat16)
    values = raw_value.astype(jnp.bfloat16)
    scores = product_of("sthd,suhd->shtu", queries, key_rows)
    weights = (scores * decay_mask[None]).astype(jnp.bfloat16)
    mixed = product_of("shtu,suhd->sthd", weights, values)
    mean_square = jnp.mean(mixed * mixed, axis=-1, keepdims=True)
    active = jnp.where(mean_square > NORM_FLOOR, 1.0, 0.0)
    inverse = lax.rsqrt(jnp.maximum(mean_square, NORM_FLOOR))
    gain_heads = norm_gain.reshape(head_count, -1)
    attended = (mixed * inverse * gain_heads).astype(jnp.bfloat16)
    return (
        attended,
        (raw_query, raw_key, queries, key_rows, values, weights, mixed, inverse, active),
    )


def attend_back(grad_attended, stashed, decay_mask, norm_gain):
    raw_query, raw_key, queries, key_rows, values, weights, mixed, inverse, active = stashed
    gain_heads = norm_gain.reshape(decay_mask.shape[0], -1)
    scaled = grad_attended * gain_heads
    grad_mixed = inverse * scaled - active * mixed * (inverse * inverse * inverse) * jnp.mean(
        scaled * mixed, axis=-1, keepdims=True
    )
    grad_mixed = grad_mixed.astype(jnp.bfloat16)
    grad_weights = product_of("sthd,suhd->shtu", grad_mixed, values)
    grad_values = product_of("shtu,sthd->suhd", weights, grad_mixed)
    grad_scores = (grad_weights * decay_mask[None]).astype(jnp.bfloat16)
    grad_query = product_of("shtu,suhd->sthd", grad_scores, key_rows)
    grad_key = product_of("shtu,sthd->suhd", grad_scores, queries)
    sigma_query = jax.nn.sigmoid(raw_query)
    sigma_key = jax.nn.sigmoid(raw_key)
    grad_query = grad_query * sigma_query * (1.0 + raw_query * (1.0 - sigma_query))
    grad_key = grad_key * sigma_key * (1.0 + raw_key * (1.0 - sigma_key))
    return grad_query, grad_key, grad_values


def adam_step(weight, first_moment, second_moment, gradient):
    first_new = BETA_ONE * first_moment + (1.0 - BETA_ONE) * gradient
    second_new = BETA_TWO * second_moment + (1.0 - BETA_TWO) * gradient * gradient
    update = first_new / BIAS_ONE / (jnp.sqrt(second_new / BIAS_TWO) + ADAM_EPS)
    weight_new = weight - LEARN_RATE * (update + WEIGHT_DECAY * weight)
    return (weight_new.astype(jnp.bfloat16), first_new)


def swap(value, axis, distance):
    count = lax.axis_size(axis)
    return lax.ppermute(value, axis, [(i, i ^ distance) for i in range(count)])


def grouping(count):
    core = 2
    inner = 2
    return count // (core * inner), inner, core


def relative_order(count):
    outer, inner, core = grouping(count)
    return [
        k * inner * core + j * core + l
        for l in range(core)
        for j in range(inner)
        for k in range(outer)
    ]


def move_block(table_ref, source_ref, target_ref):
    target_ref[...] = source_ref[...]


def reorder(source, table):
    rows, width = source.shape
    count = table.shape[0]
    block = width // count
    if block % 128:
        return jnp.take(source.reshape(rows, count, block), table, axis=1).reshape(rows, width)
    return pl.pallas_call(
        move_block,
        grid_spec=pltpu.PrefetchScalarGridSpec(
            num_scalar_prefetch=1,
            grid=(count,),
            in_specs=[pl.BlockSpec((rows, block), lambda p, table_ref: (0, table_ref[p]))],
            out_specs=pl.BlockSpec((rows, block), lambda p, table_ref: (0, p)),
        ),
        out_shape=jax.ShapeDtypeStruct(source.shape, source.dtype),
        cost_estimate=pl.CostEstimate(
            flops=0, bytes_accessed=2 * source.size * source.dtype.itemsize, transcendentals=0
        ),
    )(table, source)


def gather(piece):
    outer, inner, core = grouping(lax.axis_size("helper"))
    held = jnp.concatenate(
        [piece] + [swap(piece, "helper", k * inner * core) for k in range(1, outer)], axis=0
    )
    held = jnp.concatenate(
        [held] + [swap(held, "helper", j * core) for j in range(1, inner)], axis=0
    )
    return jnp.concatenate([held, swap(held, "helper", 1)], axis=0)


def scatter(own_columns, other_columns, right):
    outer, inner, core = grouping(lax.axis_size("helper"))
    form = (((0,), (0,)), ((), ()))
    other = lax.dot_general(other_columns, right, form, preferred_element_type=jnp.float32)
    came = swap(other.astype(jnp.bfloat16), "helper", 1)
    own = lax.dot_general(own_columns, right, form, preferred_element_type=jnp.float32)
    total = own + came
    total = total.reshape(inner, total.shape[0] // inner, -1)
    kept = total[0]
    for j in range(1, inner):
        kept = kept + swap(total[j].astype(jnp.bfloat16), "helper", j * core)
    kept = kept.reshape(outer, kept.shape[0] // outer, -1)
    last = kept[0]
    for k in range(1, outer):
        last = last + swap(kept[k].astype(jnp.bfloat16), "helper", k * inner * core)
    return last


def local(
    recorded_input_rows,
    out_cotangent,
    fresh_rows,
    seq_counts,
    decay_logs,
    norm_gain,
    qkv_weight,
    emitted_projection_matrix,
    qkv_first,
    qkv_second,
    out_first,
    out_second,
):
    local_width = qkv_weight.shape[2]
    head_count = decay_logs.shape[0]
    head_width = local_width // head_count
    helper_total = lax.axis_size("helper")
    helper = lax.axis_index("helper")
    relative = relative_order(helper_total)
    back = [relative.index(r) for r in range(helper_total)]
    table = helper ^ jnp.array(relative, jnp.int32)
    back_table = jnp.sum(
        jnp.where(
            (jnp.arange(helper_total)[:, None] ^ helper) == jnp.arange(helper_total)[None, :],
            jnp.array(back, jnp.int32)[None, :],
            0,
        ),
        axis=1,
    ).astype(jnp.int32)

    old_out = gather(emitted_projection_matrix.astype(jnp.bfloat16))
    old_qkv = [gather(qkv_weight[:, m].astype(jnp.bfloat16)) for m in range(3)]
    logged = reorder(recorded_input_rows, table)
    cotangent = reorder(out_cotangent, table)
    fresh = reorder(fresh_rows, table)

    decay_mask = decay_table(decay_logs)
    own_count = jnp.sum(jnp.where(jnp.arange(helper_total) == helper, seq_counts, 0))
    live_rows = (jnp.arange(logged.shape[0]) // SEQ_LEN < own_count)[:, None]

    def heads_of(rows, weight):
        product = jnp.dot(rows, weight, preferred_element_type=jnp.float32)
        return product.reshape(-1, SEQ_LEN, head_count, head_width)

    raw = [heads_of(logged, weight) for weight in old_qkv]
    attended, stashed = attend(*raw, decay_mask, norm_gain)
    half = logged.shape[1] // 2
    attended_rows = attended.reshape(-1, local_width)
    attended_rows = jnp.where(live_rows, attended_rows, jnp.zeros_like(attended_rows))
    out_grad = scatter(cotangent[:, :half], cotangent[:, half:], attended_rows)
    grads = attend_back(heads_of(cotangent, old_out), stashed, decay_mask, norm_gain)

    def logged_grad(grad):
        grad = jnp.where(live_rows, grad.reshape(-1, local_width), 0.0).astype(jnp.bfloat16)
        return scatter(logged[:, :half], logged[:, half:], grad)

    new_out, out_moment = adam_step(emitted_projection_matrix, out_first, out_second, out_grad)
    new_out = gather(new_out)
    new_qkv, moments = [None] * 3, [None] * 3
    for m in (2, 0, 1):
        piece, moments[m] = adam_step(
            qkv_weight[:, m], qkv_first[:, m], qkv_second[:, m], logged_grad(grads[m])
        )
        new_qkv[m] = gather(piece)
    qkv_moment = jnp.stack(moments, axis=1)

    fresh_raw = [heads_of(fresh, weight) for weight in new_qkv]
    fresh_att = attend(*fresh_raw, decay_mask, norm_gain)[0].reshape(-1, local_width)
    partial_out = lax.dot_general(
        fresh_att, new_out, (((1,), (1,)), ((), ())), preferred_element_type=jnp.float32
    )
    fresh_out = finish(partial_out, fresh)
    return (reorder(fresh_out, back_table), qkv_moment, out_moment)


def finish(partial_out, fresh):
    if lax.axis_size("tensor") == 2:
        width = partial_out.shape[1] // 2
        first = lax.axis_index("tensor") == 0
        left, right = partial_out[:, :width], partial_out[:, width:]
        came = swap(jnp.where(first, right, left).astype(jnp.bfloat16), "tensor", 1)
        residual = jnp.where(first, fresh[:, :width], fresh[:, width:])
        piece = residual.astype(jnp.float32) + (jnp.where(first, left, right) + came)
        piece = piece.astype(jnp.bfloat16)
        other = swap(piece, "tensor", 1)
        return jnp.concatenate(
            [jnp.where(first, piece, other), jnp.where(first, other, piece)], axis=1
        )
    share_sum = lax.psum_scatter(partial_out, "tensor", scatter_dimension=1, tiled=True)
    width = share_sum.shape[1]
    residual = lax.dynamic_slice_in_dim(fresh, lax.axis_index("tensor") * width, width, 1)
    piece = (residual.astype(jnp.float32) + share_sum).astype(jnp.bfloat16)
    return lax.all_gather(piece, "tensor", axis=1, tiled=True)


def solution(mesh):
    return jax.shard_map(
        local,
        mesh=mesh,
        in_specs=(
            P("helper", None),
            P("helper", None),
            P("helper", None),
            P(),
            P("tensor", None),
            P("tensor"),
            P("helper", None, "tensor"),
            P("helper", "tensor"),
            P("helper", None, "tensor"),
            P("helper", None, "tensor"),
            P("helper", "tensor"),
            P("helper", "tensor"),
        ),
        out_specs=(P("helper", None), P("helper", None, "tensor"), P("helper", "tensor")),
        check_vma=False,
    )
```

```python
import functools

import jax
import jax.numpy as jnp
from jax import lax
from jax.experimental import pallas as pl
from jax.experimental.pallas import tpu as pltpu
from jax.sharding import PartitionSpec as P


SEQ_LEN = 256


NORM_FLOOR = 1.0
BETA_ONE = 0.9
BETA_TWO = 0.95
ADAM_EPS = 1e-08
LEARN_RATE = 0.005
WEIGHT_DECAY = 0.1
BIAS_ONE = 0.9999734386011124
BIAS_TWO = 0.994079470779666


def product_of(form, left, right):
    return jnp.einsum(form, left, right, preferred_element_type=jnp.float32)


def decay_table(decay_logs):
    running = jnp.cumsum(decay_logs, axis=1)
    length = decay_logs.shape[1]
    later = (jnp.arange(length)[:, None] >= jnp.arange(length)[None, :])[None]
    spread_factor = running[:, :, None] - running[:, None, :]
    return jnp.where(later, jnp.exp(jnp.where(later, spread_factor, 0.0)), 0.0)


def attend(raw_query, raw_key, raw_value, decay_mask, norm_gain):
    head_count = decay_mask.shape[0]
    queries = (raw_query * jax.nn.sigmoid(raw_query)).astype(jnp.bfloat16)
    key_rows = (raw_key * jax.nn.sigmoid(raw_key)).astype(jnp.bfloat16)
    values = raw_value.astype(jnp.bfloat16)
    scores = product_of("sthd,suhd->shtu", queries, key_rows)
    weights = (scores * decay_mask[None]).astype(jnp.bfloat16)
    mixed = product_of("shtu,suhd->sthd", weights, values)
    mean_square = jnp.mean(mixed * mixed, axis=-1, keepdims=True)
    active = jnp.where(mean_square > NORM_FLOOR, 1.0, 0.0)
    inverse = lax.rsqrt(jnp.maximum(mean_square, NORM_FLOOR))
    gain_heads = norm_gain.reshape(head_count, -1)
    attended = (mixed * inverse * gain_heads).astype(jnp.bfloat16)
    return (
        attended,
        (raw_query, raw_key, queries, key_rows, values, weights, mixed, inverse, active),
    )


def attend_back(grad_attended, stashed, decay_mask, norm_gain):
    raw_query, raw_key, queries, key_rows, values, weights, mixed, inverse, active = stashed
    gain_heads = norm_gain.reshape(decay_mask.shape[0], -1)
    scaled = grad_attended * gain_heads
    grad_mixed = inverse * scaled - active * mixed * (inverse * inverse * inverse) * jnp.mean(
        scaled * mixed, axis=-1, keepdims=True
    )
    grad_mixed = grad_mixed.astype(jnp.bfloat16)
    grad_weights = product_of("sthd,suhd->shtu", grad_mixed, values)
    grad_values = product_of("shtu,sthd->suhd", weights, grad_mixed)
    grad_scores = (grad_weights * decay_mask[None]).astype(jnp.bfloat16)
    grad_query = product_of("shtu,suhd->sthd", grad_scores, key_rows)
    grad_key = product_of("shtu,sthd->suhd", grad_scores, queries)
    sigma_query = jax.nn.sigmoid(raw_query)
    sigma_key = jax.nn.sigmoid(raw_key)
    grad_query = grad_query * sigma_query * (1.0 + raw_query * (1.0 - sigma_query))
    grad_key = grad_key * sigma_key * (1.0 + raw_key * (1.0 - sigma_key))
    return grad_query, grad_key, grad_values


def adam_step(weight, first_moment, second_moment, gradient):
    first_new = BETA_ONE * first_moment + (1.0 - BETA_ONE) * gradient
    second_new = BETA_TWO * second_moment + (1.0 - BETA_TWO) * gradient * gradient
    update = first_new / BIAS_ONE / (jnp.sqrt(second_new / BIAS_TWO) + ADAM_EPS)
    weight_new = weight - LEARN_RATE * (update + WEIGHT_DECAY * weight)
    return (weight_new.astype(jnp.bfloat16), first_new)


def swap(value, axis, distance):
    count = lax.axis_size(axis)
    return lax.ppermute(value, axis, [(i, i ^ distance) for i in range(count)])


def grouping(count):
    core = 2
    inner = 2
    return count // (core * inner), inner, core


def relative_order(count):
    outer, inner, core = grouping(count)
    return [
        k * inner * core + j * core + l
        for l in range(core)
        for j in range(inner)
        for k in range(outer)
    ]


def move_blocks(block, count, table_ref, source_ref, target_ref):
    for p in range(count):
        start = pl.multiple_of(table_ref[p] * block, block)
        target_ref[:, p * block : (p + 1) * block] = source_ref[:, pl.ds(start, block)]


def reorder(source, table):
    rows, width = source.shape
    count = table.shape[0]
    block = width // count
    if block % 128:
        return jnp.take(source.reshape(rows, count, block), table, axis=1).reshape(rows, width)
    step = SEQ_LEN
    return pl.pallas_call(
        functools.partial(move_blocks, block, count),
        grid_spec=pltpu.PrefetchScalarGridSpec(
            num_scalar_prefetch=1,
            grid=(rows // step,),
            in_specs=[pl.BlockSpec((step, width), lambda p, table_ref: (p, 0))],
            out_specs=pl.BlockSpec((step, width), lambda p, table_ref: (p, 0)),
        ),
        out_shape=jax.ShapeDtypeStruct(source.shape, source.dtype),
        cost_estimate=pl.CostEstimate(
            flops=0, bytes_accessed=2 * source.size * source.dtype.itemsize, transcendentals=0
        ),
    )(table, source)


def gather_kernel(count, helper_total, *refs):
    pieces, fulls = refs[:count], refs[count : 2 * count]
    own_sem, z_send, z_recv, x_send, x_recv, c_send, c_recv = refs[2 * count :]
    outer, inner, core = grouping(helper_total)
    helper = lax.axis_index("helper")
    z = helper // (inner * core)
    x = (helper // core) % inner
    c = helper % core

    def at(zz, xx, cc):
        return (zz * inner + xx) * core + cc

    z_peer = [None] + [at((z + k) % outer, x, c) for k in range(1, outer)]
    x_peer = [None] + [at(z, (x + j) % inner, c) for j in range(1, inner)]
    c_peer = at(z, x, 1 - c)

    barrier = pltpu.get_barrier_semaphore()
    peers = z_peer[1:] + x_peer[1:] + [c_peer]
    for peer in peers:
        pl.semaphore_signal(
            barrier, inc=1, device_id={"helper": peer}, device_id_type=pl.DeviceIdType.MESH
        )
    pl.semaphore_wait(barrier, len(peers))

    def rows(q, owner):
        size = pieces[q].shape[0]
        return fulls[q].at[pl.ds(pl.multiple_of(owner * size, size), size)]

    def remote(source, target, send, recv, peer):
        return pltpu.make_async_remote_copy(
            src_ref=source,
            dst_ref=target,
            send_sem=send,
            recv_sem=recv,
            device_id={"helper": peer},
            device_id_type=pl.DeviceIdType.MESH,
        )

    def from_z(k):
        return at((z + outer - k) % outer, x, c)

    def z_copy(q, k):
        return remote(pieces[q], rows(q, helper), z_send.at[q, k], z_recv.at[q, k], z_peer[k])

    def x_copy(q, j, k):
        owner = from_z(k) if k else helper
        source = rows(q, owner) if k else pieces[q]
        slot = j * outer + k
        return remote(source, rows(q, owner), x_send.at[q, slot], x_recv.at[q, slot], x_peer[j])

    def c_copy(q, j, k):
        if j == 0 and k == 0:
            source, owner = pieces[q], helper
        else:
            owner = at((z + outer - k) % outer, (x + inner - j) % inner, c)
            source = rows(q, owner)
        slot = j * outer + k
        return remote(source, rows(q, owner), c_send.at[q, slot], c_recv.at[q, slot], c_peer)

    own = [pltpu.make_async_copy(pieces[q], rows(q, helper), own_sem.at[q]) for q in range(count)]
    for q in range(count):
        for k in range(1, outer):
            z_copy(q, k).start()
        for j in range(1, inner):
            x_copy(q, j, 0).start()
        own[q].start()
        c_copy(q, 0, 0).start()

    def take_x(q):
        for k in range(outer):
            for j in range(1, inner):
                x_copy(q, j, k).wait_recv()
                c_copy(q, j, k).start()

    for q in range(count):
        for k in range(1, outer):
            z_copy(q, k).wait_recv()
            for j in range(1, inner):
                x_copy(q, j, k).start()
            c_copy(q, 0, k).start()
        if q:
            take_x(q - 1)
    take_x(count - 1)
    for q in range(count):
        own[q].wait()
        for k in range(outer):
            if k:
                z_copy(q, k).wait_send()
            for j in range(inner):
                if j:
                    x_copy(q, j, k).wait_send()
                c_copy(q, j, k).wait()


def gather(pieces, identity):
    helper_total = lax.axis_size("helper")
    outer, inner, core = grouping(helper_total)
    count = len(pieces)
    semaphores = pltpu.SemaphoreType.DMA
    return pl.pallas_call(
        functools.partial(gather_kernel, count, helper_total),
        out_shape=[
            jax.ShapeDtypeStruct((piece.shape[0] * helper_total, piece.shape[1]), piece.dtype)
            for piece in pieces
        ],
        in_specs=[pl.BlockSpec(memory_space=pltpu.VMEM)] * count,
        out_specs=[pl.BlockSpec(memory_space=pl.ANY)] * count,
        scratch_shapes=[
            semaphores((count,)),
            semaphores((count, outer)),
            semaphores((count, outer)),
            semaphores((count, inner * outer)),
            semaphores((count, inner * outer)),
            semaphores((count, inner * outer)),
            semaphores((count, inner * outer)),
        ],
        compiler_params=pltpu.CompilerParams(collective_id=identity, has_side_effects=True),
    )(*pieces)


def scatter(own_columns, other_columns, right):
    outer, inner, core = grouping(lax.axis_size("helper"))
    form = (((0,), (0,)), ((), ()))
    other = lax.dot_general(other_columns, right, form, preferred_element_type=jnp.float32)
    came = swap(other.astype(jnp.bfloat16), "helper", 1)
    own = lax.dot_general(own_columns, right, form, preferred_element_type=jnp.float32)
    total = own + came
    total = total.reshape(inner, total.shape[0] // inner, -1)
    kept = total[0]
    for j in range(1, inner):
        kept = kept + swap(total[j].astype(jnp.bfloat16), "helper", j * core)
    kept = kept.reshape(outer, kept.shape[0] // outer, -1)
    last = kept[0]
    for k in range(1, outer):
        last = last + swap(kept[k].astype(jnp.bfloat16), "helper", k * inner * core)
    return last


def local(
    recorded_input_rows,
    out_cotangent,
    fresh_rows,
    seq_counts,
    decay_logs,
    norm_gain,
    qkv_weight,
    emitted_projection_matrix,
    qkv_first,
    qkv_second,
    out_first,
    out_second,
):
    local_width = qkv_weight.shape[2]
    head_count = decay_logs.shape[0]
    head_width = local_width // head_count
    helper_total = lax.axis_size("helper")
    helper = lax.axis_index("helper")
    relative = relative_order(helper_total)
    table = helper ^ jnp.array(relative, jnp.int32)
    *old_qkv, old_out = gather(
        [qkv_weight[:, m].astype(jnp.bfloat16) for m in range(3)]
        + [emitted_projection_matrix.astype(jnp.bfloat16)],
        0,
    )
    logged = reorder(recorded_input_rows, table)
    cotangent = reorder(out_cotangent, table)

    decay_mask = decay_table(decay_logs)
    own_count = jnp.sum(jnp.where(jnp.arange(helper_total) == helper, seq_counts, 0))
    live_rows = (jnp.arange(recorded_input_rows.shape[0]) // SEQ_LEN < own_count)[:, None]

    def heads_of(rows, weight):
        product = jnp.dot(rows, weight, preferred_element_type=jnp.float32)
        return product.reshape(-1, SEQ_LEN, head_count, head_width)

    raw = [heads_of(recorded_input_rows, weight) for weight in old_qkv]
    attended, stashed = attend(*raw, decay_mask, norm_gain)
    half = logged.shape[1] // 2
    attended_rows = attended.reshape(-1, local_width)
    attended_rows = jnp.where(live_rows, attended_rows, jnp.zeros_like(attended_rows))
    out_grad = scatter(cotangent[:, :half], cotangent[:, half:], attended_rows)
    grads = attend_back(heads_of(out_cotangent, old_out), stashed, decay_mask, norm_gain)

    def logged_grad(grad):
        grad = jnp.where(live_rows, grad.reshape(-1, local_width), 0.0).astype(jnp.bfloat16)
        return scatter(logged[:, :half], logged[:, half:], grad)

    new_out, out_moment = adam_step(emitted_projection_matrix, out_first, out_second, out_grad)
    pieces, moments = [None] * 3, [None] * 3
    for m in (2, 0, 1):
        pieces[m], moments[m] = adam_step(
            qkv_weight[:, m], qkv_first[:, m], qkv_second[:, m], logged_grad(grads[m])
        )
    qkv_moment = jnp.stack(moments, axis=1)

    *new_qkv, new_out = gather(pieces + [new_out], 1)
    fresh_raw = [heads_of(fresh_rows, weight) for weight in new_qkv]
    fresh_att = attend(*fresh_raw, decay_mask, norm_gain)[0].reshape(-1, local_width)
    partial_out = lax.dot_general(
        fresh_att, new_out, (((1,), (1,)), ((), ())), preferred_element_type=jnp.float32
    )
    fresh_out = finish(partial_out, fresh_rows)
    return (fresh_out, qkv_moment, out_moment)


def finish(partial_out, fresh):
    if lax.axis_size("tensor") == 2:
        width = partial_out.shape[1] // 2
        first = lax.axis_index("tensor") == 0
        left, right = partial_out[:, :width], partial_out[:, width:]
        came = swap(jnp.where(first, right, left).astype(jnp.bfloat16), "tensor", 1)
        residual = jnp.where(first, fresh[:, :width], fresh[:, width:])
        piece = residual.astype(jnp.float32) + (jnp.where(first, left, right) + came)
        piece = piece.astype(jnp.bfloat16)
        other = swap(piece, "tensor", 1)
        return jnp.concatenate(
            [jnp.where(first, piece, other), jnp.where(first, other, piece)], axis=1
        )
    share_sum = lax.psum_scatter(partial_out, "tensor", scatter_dimension=1, tiled=True)
    width = share_sum.shape[1]
    residual = lax.dynamic_slice_in_dim(fresh, lax.axis_index("tensor") * width, width, 1)
    piece = (residual.astype(jnp.float32) + share_sum).astype(jnp.bfloat16)
    return lax.all_gather(piece, "tensor", axis=1, tiled=True)


def solution(mesh):
    return jax.shard_map(
        local,
        mesh=mesh,
        in_specs=(
            P("helper", None),
            P("helper", None),
            P("helper", None),
            P(),
            P("tensor", None),
            P("tensor"),
            P("helper", None, "tensor"),
            P("helper", "tensor"),
            P("helper", None, "tensor"),
            P("helper", None, "tensor"),
            P("helper", "tensor"),
            P("helper", "tensor"),
        ),
        out_specs=(P("helper", None), P("helper", None, "tensor"), P("helper", "tensor")),
        check_vma=False,
    )
```

```python
import functools

import jax
import jax.numpy as jnp
from jax import lax
from jax.experimental import pallas as pl
from jax.experimental.pallas import tpu as pltpu
from jax.sharding import PartitionSpec as P


SEQ_LEN = 256


NORM_FLOOR = 1.0
BETA_ONE = 0.9
BETA_TWO = 0.95
ADAM_EPS = 1e-08
LEARN_RATE = 0.005
WEIGHT_DECAY = 0.1
BIAS_ONE = 0.9999734386011124
BIAS_TWO = 0.994079470779666


def decay_table(decay_logs):
    running = jnp.cumsum(decay_logs, axis=1)
    length = decay_logs.shape[1]
    later = (jnp.arange(length)[:, None] >= jnp.arange(length)[None, :])[None]
    spread_factor = running[:, :, None] - running[:, None, :]
    return jnp.where(later, jnp.exp(jnp.where(later, spread_factor, 0.0)), 0.0)


def multiply(left, right, left_dim, right_dim):
    return lax.dot_general(
        left, right, (((left_dim,), (right_dim,)), ((), ())), preferred_element_type=jnp.float32
    )


def head_forward(raw_query, raw_key, raw_value, mask, gain):
    sigma_query = jax.nn.sigmoid(raw_query)
    sigma_key = jax.nn.sigmoid(raw_key)
    queries = (raw_query * sigma_query).astype(jnp.bfloat16)
    key_rows = (raw_key * sigma_key).astype(jnp.bfloat16)
    values = raw_value.astype(jnp.bfloat16)
    weights = (multiply(queries, key_rows, 1, 1) * mask).astype(jnp.bfloat16)
    mixed = multiply(weights, values, 1, 0)
    mean_square = jnp.mean(mixed * mixed, axis=-1, keepdims=True)
    inverse = lax.rsqrt(jnp.maximum(mean_square, NORM_FLOOR))
    attended = (mixed * inverse * gain).astype(jnp.bfloat16)
    return (
        attended,
        (sigma_query, sigma_key, queries, key_rows, values, weights, mixed, mean_square, inverse),
    )


def replay_kernel(head_width, count_ref, query, key, value, cotangent, mask, gain, *outs):
    live = pl.program_id(1) < count_ref[0]

    @pl.when(live)
    def _():
        for n in range(mask.shape[0]):
            at = slice(n * head_width, (n + 1) * head_width)
            raw_query, raw_key = query[:, at], key[:, at]
            decay = mask[n]
            gain_row = gain[:, at]
            attended, kept = head_forward(raw_query, raw_key, value[:, at], decay, gain_row)
            sigma_query, sigma_key, queries, key_rows, values, weights, mixed, square, inverse = kept
            active = jnp.where(square > NORM_FLOOR, 1.0, 0.0)
            scaled = cotangent[:, at] * gain_row
            grad_mixed = inverse * scaled - active * mixed * (
                inverse * inverse * inverse
            ) * jnp.mean(scaled * mixed, axis=-1, keepdims=True)
            grad_mixed = grad_mixed.astype(jnp.bfloat16)
            grad_scores = (multiply(grad_mixed, values, 1, 1) * decay).astype(jnp.bfloat16)
            grad_value = multiply(weights, grad_mixed, 0, 0)
            grad_query = multiply(grad_scores, key_rows, 1, 0)
            grad_key = multiply(grad_scores, queries, 0, 0)
            grad_query = grad_query * sigma_query * (1.0 + raw_query * (1.0 - sigma_query))
            grad_key = grad_key * sigma_key * (1.0 + raw_key * (1.0 - sigma_key))
            for out, result in zip(outs, (attended, grad_query, grad_key, grad_value)):
                out[:, at] = result.astype(jnp.bfloat16)

    @pl.when(jnp.logical_not(live))
    def _():
        for out in outs:
            out[...] = jnp.zeros_like(out)


def fresh_kernel(head_width, query, key, value, mask, gain, out):
    for n in range(mask.shape[0]):
        at = slice(n * head_width, (n + 1) * head_width)
        out[:, at] = head_forward(query[:, at], key[:, at], value[:, at], mask[n], gain[:, at])[0]


def head_specs(raw, mask, arrays):
    rows, width = raw.shape
    head_count = mask.shape[0]
    head_width = width // head_count
    together = 2 if head_count % 2 == 0 else 1
    block = together * head_width
    row_spec = pl.BlockSpec((SEQ_LEN, block), lambda n, s, *_: (s, n))
    specs = [row_spec] * arrays + [
        pl.BlockSpec((together, SEQ_LEN, SEQ_LEN), lambda n, s, *_: (n, 0, 0)),
        pl.BlockSpec((1, block), lambda n, s, *_: (0, n)),
    ]
    return head_width, (head_count // together, rows // SEQ_LEN), row_spec, specs


def replay_heads(raw, cotangent, mask, norm_gain, own_count):
    head_width, grid, row_spec, specs = head_specs(raw[0], mask, 4)
    shape = jax.ShapeDtypeStruct(raw[0].shape, jnp.bfloat16)
    return pl.pallas_call(
        functools.partial(replay_kernel, head_width),
        grid_spec=pltpu.PrefetchScalarGridSpec(
            num_scalar_prefetch=1, grid=grid, in_specs=specs, out_specs=[row_spec] * 4
        ),
        out_shape=[shape] * 4,
    )(own_count.reshape(1), *raw, cotangent, mask, norm_gain.reshape(1, -1))


def fresh_heads(raw, mask, norm_gain):
    head_width, grid, row_spec, specs = head_specs(raw[0], mask, 3)
    return pl.pallas_call(
        functools.partial(fresh_kernel, head_width),
        grid=grid,
        in_specs=specs,
        out_specs=row_spec,
        out_shape=jax.ShapeDtypeStruct(raw[0].shape, jnp.bfloat16),
    )(*raw, mask, norm_gain.reshape(1, -1))


def adam_step(weight, first_moment, second_moment, gradient):
    first_new = BETA_ONE * first_moment + (1.0 - BETA_ONE) * gradient
    second_new = BETA_TWO * second_moment + (1.0 - BETA_TWO) * gradient * gradient
    update = first_new / BIAS_ONE / (jnp.sqrt(second_new / BIAS_TWO) + ADAM_EPS)
    weight_new = weight - LEARN_RATE * (update + WEIGHT_DECAY * weight)
    return (weight_new.astype(jnp.bfloat16), first_new)


def swap(value, axis, distance):
    count = lax.axis_size(axis)
    return lax.ppermute(value, axis, [(i, i ^ distance) for i in range(count)])


def grouping(count):
    core = 2
    inner = 2
    return count // (core * inner), inner, core


def relative_order(count):
    outer, inner, core = grouping(count)
    return [
        k * inner * core + j * core + l
        for l in range(core)
        for j in range(inner)
        for k in range(outer)
    ]


def move_blocks(block, count, table_ref, source_ref, target_ref):
    for p in range(count):
        start = pl.multiple_of(table_ref[p] * block, block)
        target_ref[:, p * block : (p + 1) * block] = source_ref[:, pl.ds(start, block)]


def reorder(source, table):
    rows, width = source.shape
    count = table.shape[0]
    block = width // count
    if block % 128:
        return jnp.take(source.reshape(rows, count, block), table, axis=1).reshape(rows, width)
    step = SEQ_LEN
    return pl.pallas_call(
        functools.partial(move_blocks, block, count),
        grid_spec=pltpu.PrefetchScalarGridSpec(
            num_scalar_prefetch=1,
            grid=(rows // step,),
            in_specs=[pl.BlockSpec((step, width), lambda p, table_ref: (p, 0))],
            out_specs=pl.BlockSpec((step, width), lambda p, table_ref: (p, 0)),
        ),
        out_shape=jax.ShapeDtypeStruct(source.shape, source.dtype),
        cost_estimate=pl.CostEstimate(
            flops=0, bytes_accessed=2 * source.size * source.dtype.itemsize, transcendentals=0
        ),
    )(table, source)


def gather_kernel(count, helper_total, *refs):
    pieces, fulls = refs[:count], refs[count : 2 * count]
    own_sem, z_send, z_recv, x_send, x_recv, c_send, c_recv = refs[2 * count :]
    outer, inner, core = grouping(helper_total)
    helper = lax.axis_index("helper")
    z = helper // (inner * core)
    x = (helper // core) % inner
    c = helper % core

    def at(zz, xx, cc):
        return (zz * inner + xx) * core + cc

    z_peer = [None] + [at((z + k) % outer, x, c) for k in range(1, outer)]
    x_peer = [None] + [at(z, (x + j) % inner, c) for j in range(1, inner)]
    c_peer = at(z, x, 1 - c)

    barrier = pltpu.get_barrier_semaphore()
    peers = z_peer[1:] + x_peer[1:] + [c_peer]
    for peer in peers:
        pl.semaphore_signal(
            barrier, inc=1, device_id={"helper": peer}, device_id_type=pl.DeviceIdType.MESH
        )
    pl.semaphore_wait(barrier, len(peers))

    def rows(q, owner):
        size = pieces[q].shape[0]
        return fulls[q].at[pl.ds(pl.multiple_of(owner * size, size), size)]

    def remote(source, target, send, recv, peer):
        return pltpu.make_async_remote_copy(
            src_ref=source,
            dst_ref=target,
            send_sem=send,
            recv_sem=recv,
            device_id={"helper": peer},
            device_id_type=pl.DeviceIdType.MESH,
        )

    def from_z(k):
        return at((z + outer - k) % outer, x, c)

    def z_copy(q, k):
        return remote(pieces[q], rows(q, helper), z_send.at[q, k], z_recv.at[q, k], z_peer[k])

    def x_copy(q, j, k):
        owner = from_z(k) if k else helper
        source = rows(q, owner) if k else pieces[q]
        slot = j * outer + k
        return remote(source, rows(q, owner), x_send.at[q, slot], x_recv.at[q, slot], x_peer[j])

    def c_copy(q, j, k):
        if j == 0 and k == 0:
            source, owner = pieces[q], helper
        else:
            owner = at((z + outer - k) % outer, (x + inner - j) % inner, c)
            source = rows(q, owner)
        slot = j * outer + k
        return remote(source, rows(q, owner), c_send.at[q, slot], c_recv.at[q, slot], c_peer)

    own = [pltpu.make_async_copy(pieces[q], rows(q, helper), own_sem.at[q]) for q in range(count)]
    for q in range(count):
        for k in range(1, outer):
            z_copy(q, k).start()
        for j in range(1, inner):
            x_copy(q, j, 0).start()
        own[q].start()
        c_copy(q, 0, 0).start()

    def take_x(q):
        for k in range(outer):
            for j in range(1, inner):
                x_copy(q, j, k).wait_recv()
                c_copy(q, j, k).start()

    for q in range(count):
        for k in range(1, outer):
            z_copy(q, k).wait_recv()
            for j in range(1, inner):
                x_copy(q, j, k).start()
            c_copy(q, 0, k).start()
        if q:
            take_x(q - 1)
    take_x(count - 1)
    for q in range(count):
        own[q].wait()
        for k in range(outer):
            if k:
                z_copy(q, k).wait_send()
            for j in range(inner):
                if j:
                    x_copy(q, j, k).wait_send()
                c_copy(q, j, k).wait()


def gather(pieces, identity):
    helper_total = lax.axis_size("helper")
    outer, inner, core = grouping(helper_total)
    count = len(pieces)
    semaphores = pltpu.SemaphoreType.DMA
    return pl.pallas_call(
        functools.partial(gather_kernel, count, helper_total),
        out_shape=[
            jax.ShapeDtypeStruct((piece.shape[0] * helper_total, piece.shape[1]), piece.dtype)
            for piece in pieces
        ],
        in_specs=[pl.BlockSpec(memory_space=pltpu.VMEM)] * count,
        out_specs=[pl.BlockSpec(memory_space=pl.ANY)] * count,
        scratch_shapes=[
            semaphores((count,)),
            semaphores((count, outer)),
            semaphores((count, outer)),
            semaphores((count, inner * outer)),
            semaphores((count, inner * outer)),
            semaphores((count, inner * outer)),
            semaphores((count, inner * outer)),
        ],
        compiler_params=pltpu.CompilerParams(collective_id=identity, has_side_effects=True),
    )(*pieces)


def scatter(own_columns, other_columns, right):
    outer, inner, core = grouping(lax.axis_size("helper"))
    form = (((0,), (0,)), ((), ()))
    other = lax.dot_general(other_columns, right, form, preferred_element_type=jnp.float32)
    came = swap(other.astype(jnp.bfloat16), "helper", 1)
    own = lax.dot_general(own_columns, right, form, preferred_element_type=jnp.float32)
    total = own + came
    total = total.reshape(inner, total.shape[0] // inner, -1)
    kept = total[0]
    for j in range(1, inner):
        kept = kept + swap(total[j].astype(jnp.bfloat16), "helper", j * core)
    kept = kept.reshape(outer, kept.shape[0] // outer, -1)
    last = kept[0]
    for k in range(1, outer):
        last = last + swap(kept[k].astype(jnp.bfloat16), "helper", k * inner * core)
    return last


def local(
    recorded_input_rows,
    out_cotangent,
    fresh_rows,
    seq_counts,
    decay_logs,
    norm_gain,
    qkv_weight,
    emitted_projection_matrix,
    qkv_first,
    qkv_second,
    out_first,
    out_second,
):
    helper_total = lax.axis_size("helper")
    helper = lax.axis_index("helper")
    relative = relative_order(helper_total)
    table = helper ^ jnp.array(relative, jnp.int32)
    *old_qkv, old_out = gather(
        [qkv_weight[:, m].astype(jnp.bfloat16) for m in range(3)]
        + [emitted_projection_matrix.astype(jnp.bfloat16)],
        0,
    )
    logged = reorder(recorded_input_rows, table)
    cotangent = reorder(out_cotangent, table)

    decay_mask = decay_table(decay_logs)
    own_count = jnp.sum(jnp.where(jnp.arange(helper_total) == helper, seq_counts, 0))

    def product(rows, weight):
        return jnp.dot(rows, weight, preferred_element_type=jnp.float32)

    half = logged.shape[1] // 2
    attended, *grads = replay_heads(
        [product(recorded_input_rows, weight) for weight in old_qkv],
        product(out_cotangent, old_out),
        decay_mask,
        norm_gain,
        own_count,
    )
    out_grad = scatter(cotangent[:, :half], cotangent[:, half:], attended)

    def logged_grad(grad):
        return scatter(logged[:, :half], logged[:, half:], grad)

    new_out, out_moment = adam_step(emitted_projection_matrix, out_first, out_second, out_grad)
    pieces, moments = [None] * 3, [None] * 3
    for m in (2, 0, 1):
        pieces[m], moments[m] = adam_step(
            qkv_weight[:, m], qkv_first[:, m], qkv_second[:, m], logged_grad(grads[m])
        )
    qkv_moment = jnp.stack(moments, axis=1)

    *new_qkv, new_out = gather(pieces + [new_out], 1)
    fresh_raw = [product(fresh_rows, weight) for weight in new_qkv]
    fresh_att = fresh_heads(fresh_raw, decay_mask, norm_gain)
    partial_out = lax.dot_general(
        fresh_att, new_out, (((1,), (1,)), ((), ())), preferred_element_type=jnp.float32
    )
    fresh_out = finish(partial_out, fresh_rows)
    return (fresh_out, qkv_moment, out_moment)


def finish(partial_out, fresh):
    if lax.axis_size("tensor") == 2:
        width = partial_out.shape[1] // 2
        first = lax.axis_index("tensor") == 0
        left, right = partial_out[:, :width], partial_out[:, width:]
        came = swap(jnp.where(first, right, left).astype(jnp.bfloat16), "tensor", 1)
        residual = jnp.where(first, fresh[:, :width], fresh[:, width:])
        piece = residual.astype(jnp.float32) + (jnp.where(first, left, right) + came)
        piece = piece.astype(jnp.bfloat16)
        other = swap(piece, "tensor", 1)
        return jnp.concatenate(
            [jnp.where(first, piece, other), jnp.where(first, other, piece)], axis=1
        )
    share_sum = lax.psum_scatter(partial_out, "tensor", scatter_dimension=1, tiled=True)
    width = share_sum.shape[1]
    residual = lax.dynamic_slice_in_dim(fresh, lax.axis_index("tensor") * width, width, 1)
    piece = (residual.astype(jnp.float32) + share_sum).astype(jnp.bfloat16)
    return lax.all_gather(piece, "tensor", axis=1, tiled=True)


def solution(mesh):
    return jax.shard_map(
        local,
        mesh=mesh,
        in_specs=(
            P("helper", None),
            P("helper", None),
            P("helper", None),
            P(),
            P("tensor", None),
            P("tensor"),
            P("helper", None, "tensor"),
            P("helper", "tensor"),
            P("helper", None, "tensor"),
            P("helper", None, "tensor"),
            P("helper", "tensor"),
            P("helper", "tensor"),
        ),
        out_specs=(P("helper", None), P("helper", None, "tensor"), P("helper", "tensor")),
        check_vma=False,
    )
```

```python
import functools

import jax
import jax.numpy as jnp
from jax import lax
from jax.experimental import pallas as pl
from jax.experimental.pallas import tpu as pltpu
from jax.sharding import PartitionSpec as P


SEQ_LEN = 256


NORM_FLOOR = 1.0
BETA_ONE = 0.9
BETA_TWO = 0.95
ADAM_EPS = 1e-08
LEARN_RATE = 0.005
WEIGHT_DECAY = 0.1
BIAS_ONE = 0.9999734386011124
BIAS_TWO = 0.994079470779666


def decay_table(decay_logs):
    running = jnp.cumsum(decay_logs, axis=1)
    length = decay_logs.shape[1]
    later = (jnp.arange(length)[:, None] >= jnp.arange(length)[None, :])[None]
    spread_factor = running[:, :, None] - running[:, None, :]
    return jnp.where(later, jnp.exp(jnp.where(later, spread_factor, 0.0)), 0.0)


def multiply(left, right, left_dim, right_dim):
    return lax.dot_general(
        left, right, (((left_dim,), (right_dim,)), ((), ())), preferred_element_type=jnp.float32
    )


def head_forward(raw_query, raw_key, raw_value, mask, gain):
    sigma_query = jax.nn.sigmoid(raw_query)
    sigma_key = jax.nn.sigmoid(raw_key)
    queries = (raw_query * sigma_query).astype(jnp.bfloat16)
    key_rows = (raw_key * sigma_key).astype(jnp.bfloat16)
    values = raw_value.astype(jnp.bfloat16)
    weights = (multiply(queries, key_rows, 1, 1) * mask).astype(jnp.bfloat16)
    mixed = multiply(weights, values, 1, 0)
    mean_square = jnp.mean(mixed * mixed, axis=-1, keepdims=True)
    inverse = lax.rsqrt(jnp.maximum(mean_square, NORM_FLOOR))
    attended = (mixed * inverse * gain).astype(jnp.bfloat16)
    return (
        attended,
        (sigma_query, sigma_key, queries, key_rows, values, weights, mixed, mean_square, inverse),
    )


def replay_kernel(head_width, count_ref, query, key, value, cotangent, mask, gain, *outs):
    live = pl.program_id(1) < count_ref[0]

    @pl.when(live)
    def _():
        for n in range(mask.shape[0]):
            at = slice(n * head_width, (n + 1) * head_width)
            raw_query, raw_key = query[:, at], key[:, at]
            decay = mask[n]
            gain_row = gain[:, at]
            attended, kept = head_forward(raw_query, raw_key, value[:, at], decay, gain_row)
            sigma_query, sigma_key, queries, key_rows, values, weights, mixed, square, inverse = kept
            active = jnp.where(square > NORM_FLOOR, 1.0, 0.0)
            scaled = cotangent[:, at] * gain_row
            grad_mixed = inverse * scaled - active * mixed * (
                inverse * inverse * inverse
            ) * jnp.mean(scaled * mixed, axis=-1, keepdims=True)
            grad_mixed = grad_mixed.astype(jnp.bfloat16)
            grad_scores = (multiply(grad_mixed, values, 1, 1) * decay).astype(jnp.bfloat16)
            grad_value = multiply(weights, grad_mixed, 0, 0)
            grad_query = multiply(grad_scores, key_rows, 1, 0)
            grad_key = multiply(grad_scores, queries, 0, 0)
            grad_query = grad_query * sigma_query * (1.0 + raw_query * (1.0 - sigma_query))
            grad_key = grad_key * sigma_key * (1.0 + raw_key * (1.0 - sigma_key))
            for out, result in zip(outs, (attended, grad_query, grad_key, grad_value)):
                out[:, at] = result.astype(jnp.bfloat16)

    @pl.when(jnp.logical_not(live))
    def _():
        for out in outs:
            out[...] = jnp.zeros_like(out)


def fresh_kernel(head_width, query, key, value, mask, gain, out):
    for n in range(mask.shape[0]):
        at = slice(n * head_width, (n + 1) * head_width)
        out[:, at] = head_forward(query[:, at], key[:, at], value[:, at], mask[n], gain[:, at])[0]


def head_specs(raw, mask, arrays):
    rows, width = raw.shape
    head_count = mask.shape[0]
    head_width = width // head_count
    together = 2 if head_count % 2 == 0 else 1
    block = together * head_width
    row_spec = pl.BlockSpec((SEQ_LEN, block), lambda n, s, *_: (s, n))
    specs = [row_spec] * arrays + [
        pl.BlockSpec((together, SEQ_LEN, SEQ_LEN), lambda n, s, *_: (n, 0, 0)),
        pl.BlockSpec((1, block), lambda n, s, *_: (0, n)),
    ]
    return head_width, (head_count // together, rows // SEQ_LEN), row_spec, specs


def replay_heads(raw, cotangent, mask, norm_gain, own_count):
    head_width, grid, row_spec, specs = head_specs(raw[0], mask, 4)
    shape = jax.ShapeDtypeStruct(raw[0].shape, jnp.bfloat16)
    return pl.pallas_call(
        functools.partial(replay_kernel, head_width),
        grid_spec=pltpu.PrefetchScalarGridSpec(
            num_scalar_prefetch=1, grid=grid, in_specs=specs, out_specs=[row_spec] * 4
        ),
        out_shape=[shape] * 4,
    )(own_count.reshape(1), *raw, cotangent, mask, norm_gain.reshape(1, -1))


def fresh_heads(raw, mask, norm_gain):
    head_width, grid, row_spec, specs = head_specs(raw[0], mask, 3)
    return pl.pallas_call(
        functools.partial(fresh_kernel, head_width),
        grid=grid,
        in_specs=specs,
        out_specs=row_spec,
        out_shape=jax.ShapeDtypeStruct(raw[0].shape, jnp.bfloat16),
    )(*raw, mask, norm_gain.reshape(1, -1))


def adam_step(weight, first_moment, second_moment, gradient):
    first_new = BETA_ONE * first_moment + (1.0 - BETA_ONE) * gradient
    second_new = BETA_TWO * second_moment + (1.0 - BETA_TWO) * gradient * gradient
    update = first_new / BIAS_ONE / (jnp.sqrt(second_new / BIAS_TWO) + ADAM_EPS)
    weight_new = weight - LEARN_RATE * (update + WEIGHT_DECAY * weight)
    return (weight_new.astype(jnp.bfloat16), first_new)


def swap(value, axis, distance):
    count = lax.axis_size(axis)
    return lax.ppermute(value, axis, [(i, i ^ distance) for i in range(count)])


def grouping(count):
    core = 2
    inner = 2
    return count // (core * inner), inner, core


def relative_order(count):
    outer, inner, core = grouping(count)
    return [
        k * inner * core + j * core + l
        for l in range(core)
        for j in range(inner)
        for k in range(outer)
    ]


def move_blocks(block, count, table_ref, source_ref, target_ref):
    for p in range(count):
        start = pl.multiple_of(table_ref[p] * block, block)
        target_ref[:, p * block : (p + 1) * block] = source_ref[:, pl.ds(start, block)]


def reorder(source, table):
    rows, width = source.shape
    count = table.shape[0]
    block = width // count
    if block % 128:
        return jnp.take(source.reshape(rows, count, block), table, axis=1).reshape(rows, width)
    step = SEQ_LEN
    return pl.pallas_call(
        functools.partial(move_blocks, block, count),
        grid_spec=pltpu.PrefetchScalarGridSpec(
            num_scalar_prefetch=1,
            grid=(rows // step,),
            in_specs=[pl.BlockSpec((step, width), lambda p, table_ref: (p, 0))],
            out_specs=pl.BlockSpec((step, width), lambda p, table_ref: (p, 0)),
        ),
        out_shape=jax.ShapeDtypeStruct(source.shape, source.dtype),
        cost_estimate=pl.CostEstimate(
            flops=0, bytes_accessed=2 * source.size * source.dtype.itemsize, transcendentals=0
        ),
    )(table, source)


def gather_kernel(count, helper_total, *refs):
    pieces, fulls = refs[:count], refs[count : 2 * count]
    own_sem, z_send, z_recv, x_send, x_recv, c_send, c_recv = refs[2 * count :]
    outer, inner, core = grouping(helper_total)
    helper = lax.axis_index("helper")
    z = helper // (inner * core)
    x = (helper // core) % inner
    c = helper % core

    def at(zz, xx, cc):
        return (zz * inner + xx) * core + cc

    z_peer = [None] + [at((z + k) % outer, x, c) for k in range(1, outer)]
    x_peer = [None] + [at(z, (x + j) % inner, c) for j in range(1, inner)]
    c_peer = at(z, x, 1 - c)

    barrier = pltpu.get_barrier_semaphore()
    peers = z_peer[1:] + x_peer[1:] + [c_peer]
    for peer in peers:
        pl.semaphore_signal(
            barrier, inc=1, device_id={"helper": peer}, device_id_type=pl.DeviceIdType.MESH
        )
    pl.semaphore_wait(barrier, len(peers))

    def rows(q, owner):
        size = pieces[q].shape[0]
        return fulls[q].at[pl.ds(pl.multiple_of(owner * size, size), size)]

    def remote(source, target, send, recv, peer):
        return pltpu.make_async_remote_copy(
            src_ref=source,
            dst_ref=target,
            send_sem=send,
            recv_sem=recv,
            device_id={"helper": peer},
            device_id_type=pl.DeviceIdType.MESH,
        )

    def from_z(k):
        return at((z + outer - k) % outer, x, c)

    def z_copy(q, k):
        return remote(pieces[q], rows(q, helper), z_send.at[q, k], z_recv.at[q, k], z_peer[k])

    def x_copy(q, j, k):
        owner = from_z(k) if k else helper
        source = rows(q, owner) if k else pieces[q]
        slot = j * outer + k
        return remote(source, rows(q, owner), x_send.at[q, slot], x_recv.at[q, slot], x_peer[j])

    def c_copy(q, j, k):
        if j == 0 and k == 0:
            source, owner = pieces[q], helper
        else:
            owner = at((z + outer - k) % outer, (x + inner - j) % inner, c)
            source = rows(q, owner)
        slot = j * outer + k
        return remote(source, rows(q, owner), c_send.at[q, slot], c_recv.at[q, slot], c_peer)

    own = [pltpu.make_async_copy(pieces[q], rows(q, helper), own_sem.at[q]) for q in range(count)]
    for q in range(count):
        for k in range(1, outer):
            z_copy(q, k).start()
        for j in range(1, inner):
            x_copy(q, j, 0).start()
        own[q].start()
        c_copy(q, 0, 0).start()

    def take_x(q):
        for k in range(outer):
            for j in range(1, inner):
                x_copy(q, j, k).wait_recv()
                c_copy(q, j, k).start()

    for q in range(count):
        for k in range(1, outer):
            z_copy(q, k).wait_recv()
            for j in range(1, inner):
                x_copy(q, j, k).start()
            c_copy(q, 0, k).start()
        if q:
            take_x(q - 1)
    take_x(count - 1)
    for q in range(count):
        own[q].wait()
        for k in range(outer):
            if k:
                z_copy(q, k).wait_send()
            for j in range(inner):
                if j:
                    x_copy(q, j, k).wait_send()
                c_copy(q, j, k).wait()


def gather(pieces, identity):
    helper_total = lax.axis_size("helper")
    outer, inner, core = grouping(helper_total)
    count = len(pieces)
    semaphores = pltpu.SemaphoreType.DMA
    return pl.pallas_call(
        functools.partial(gather_kernel, count, helper_total),
        out_shape=[
            jax.ShapeDtypeStruct((piece.shape[0] * helper_total, piece.shape[1]), piece.dtype)
            for piece in pieces
        ],
        in_specs=[pl.BlockSpec(memory_space=pltpu.VMEM)] * count,
        out_specs=[pl.BlockSpec(memory_space=pl.ANY)] * count,
        scratch_shapes=[
            semaphores((count,)),
            semaphores((count, outer)),
            semaphores((count, outer)),
            semaphores((count, inner * outer)),
            semaphores((count, inner * outer)),
            semaphores((count, inner * outer)),
            semaphores((count, inner * outer)),
        ],
        compiler_params=pltpu.CompilerParams(collective_id=identity, has_side_effects=True),
    )(*pieces)


def scatter(own_columns, other_columns, right, outer_first=False):
    outer, inner, core = grouping(lax.axis_size("helper"))
    form = (((0,), (0,)), ((), ()))
    other = lax.dot_general(other_columns, right, form, preferred_element_type=jnp.float32)
    came = swap(other.astype(jnp.bfloat16), "helper", 1)
    own = lax.dot_general(own_columns, right, form, preferred_element_type=jnp.float32)
    total = own + came
    if outer_first:
        total = total.reshape(inner, outer, total.shape[0] // (inner * outer), -1)
        kept = total[:, 0]
        for k in range(1, outer):
            kept = kept + swap(total[:, k].astype(jnp.bfloat16), "helper", k * inner * core)
        last = kept[0]
        for j in range(1, inner):
            last = last + swap(kept[j].astype(jnp.bfloat16), "helper", j * core)
        return last
    total = total.reshape(inner, total.shape[0] // inner, -1)
    kept = total[0]
    for j in range(1, inner):
        kept = kept + swap(total[j].astype(jnp.bfloat16), "helper", j * core)
    kept = kept.reshape(outer, kept.shape[0] // outer, -1)
    last = kept[0]
    for k in range(1, outer):
        last = last + swap(kept[k].astype(jnp.bfloat16), "helper", k * inner * core)
    return last


def local(
    recorded_input_rows,
    out_cotangent,
    fresh_rows,
    seq_counts,
    decay_logs,
    norm_gain,
    qkv_weight,
    emitted_projection_matrix,
    qkv_first,
    qkv_second,
    out_first,
    out_second,
):
    helper_total = lax.axis_size("helper")
    helper = lax.axis_index("helper")
    relative = relative_order(helper_total)
    table = helper ^ jnp.array(relative, jnp.int32)
    *old_qkv, old_out = gather(
        [qkv_weight[:, m].astype(jnp.bfloat16) for m in range(3)]
        + [emitted_projection_matrix.astype(jnp.bfloat16)],
        0,
    )
    logged = reorder(recorded_input_rows, table)
    cotangent = reorder(out_cotangent, table)

    decay_mask = decay_table(decay_logs)
    own_count = jnp.sum(jnp.where(jnp.arange(helper_total) == helper, seq_counts, 0))

    def product(rows, weight):
        return jnp.dot(rows, weight, preferred_element_type=jnp.float32)

    half = logged.shape[1] // 2
    attended, *grads = replay_heads(
        [product(recorded_input_rows, weight) for weight in old_qkv],
        product(out_cotangent, old_out),
        decay_mask,
        norm_gain,
        own_count,
    )
    out_grad = scatter(cotangent[:, :half], cotangent[:, half:], attended, True)

    def logged_grad(grad):
        return scatter(logged[:, :half], logged[:, half:], grad)

    new_out, out_moment = adam_step(emitted_projection_matrix, out_first, out_second, out_grad)
    pieces, moments = [None] * 3, [None] * 3
    for m in (2, 0, 1):
        pieces[m], moments[m] = adam_step(
            qkv_weight[:, m], qkv_first[:, m], qkv_second[:, m], logged_grad(grads[m])
        )
    qkv_moment = jnp.stack(moments, axis=1)

    *new_qkv, new_out = gather(pieces + [new_out], 1)
    fresh_raw = [product(fresh_rows, weight) for weight in new_qkv]
    fresh_att = fresh_heads(fresh_raw, decay_mask, norm_gain)
    partial_out = lax.dot_general(
        fresh_att, new_out, (((1,), (1,)), ((), ())), preferred_element_type=jnp.float32
    )
    fresh_out = finish(partial_out, fresh_rows)
    return (fresh_out, qkv_moment, out_moment)


def finish(partial_out, fresh):
    if lax.axis_size("tensor") == 2:
        width = partial_out.shape[1] // 2
        first = lax.axis_index("tensor") == 0
        left, right = partial_out[:, :width], partial_out[:, width:]
        came = swap(jnp.where(first, right, left).astype(jnp.bfloat16), "tensor", 1)
        residual = jnp.where(first, fresh[:, :width], fresh[:, width:])
        piece = residual.astype(jnp.float32) + (jnp.where(first, left, right) + came)
        piece = piece.astype(jnp.bfloat16)
        other = swap(piece, "tensor", 1)
        return jnp.concatenate(
            [jnp.where(first, piece, other), jnp.where(first, other, piece)], axis=1
        )
    share_sum = lax.psum_scatter(partial_out, "tensor", scatter_dimension=1, tiled=True)
    width = share_sum.shape[1]
    residual = lax.dynamic_slice_in_dim(fresh, lax.axis_index("tensor") * width, width, 1)
    piece = (residual.astype(jnp.float32) + share_sum).astype(jnp.bfloat16)
    return lax.all_gather(piece, "tensor", axis=1, tiled=True)


def solution(mesh):
    return jax.shard_map(
        local,
        mesh=mesh,
        in_specs=(
            P("helper", None),
            P("helper", None),
            P("helper", None),
            P(),
            P("tensor", None),
            P("tensor"),
            P("helper", None, "tensor"),
            P("helper", "tensor"),
            P("helper", None, "tensor"),
            P("helper", None, "tensor"),
            P("helper", "tensor"),
            P("helper", "tensor"),
        ),
        out_specs=(P("helper", None), P("helper", None, "tensor"), P("helper", "tensor")),
        check_vma=False,
    )
```
